256 devices in a mesh: dp: 32 (over x, y, core), tensor: 8 (over z).
Axes of the slice: x: 4, y: 4, z: 8, core: 2. Of those that a mesh axis runs over, the one named last changes fastest.
Arguments:
- hidden: bfloat16 [32768, 8192], P(('dp', 'tensor')), may hold values from -50 to 50
- out_weight: bfloat16 [128256, 8192], P(('dp', 'tensor')), may hold values from -1 to 1
- loss_mask: int32 [32768], P(('dp', 'tensor')), may hold values from 0 to 1, as said below
- targets: int32 [32768], P(('dp', 'tensor')), may hold values from 0 to 128255
- kept_count: int32 [256], P(('dp', 'tensor')), may hold values from 0 to 1, as said below
Outputs:
- hidden_grad: bfloat16 [32768, 8192], P(('dp', 'tensor'))
- row_loss: float32 [32768], P(('dp', 'tensor'))
The draws below stay inside these ranges and needn't reach their ends.
Inputs may be any that keep to these rules, and one draw needn't show every extreme that they name: `loss_mask`: each device's 128 rows hold at least 1 ones. `kept_count`: some entry equals 1 and some entry equals 0.
All inputs are finite; a program needn't handle non-finite values.
Results may differ from the reference program's by a relative error of at most 0.0026.
Values may be sent and summed in bfloat16 or wider, within the bound.
No kernel may reach another device: no remote copies, remote signals or barrier semaphores. Data moves between devices by JAX's collectives and lax.ppermute only.
A program may use at most 128 MiB of HBM per device.

```python
import math
import jax
import jax.numpy as jnp
import numpy as np
from jax import lax

D = 8192
VOCAB = 128256
TOK_DEV = 128
CAP = 1
ROWS = 32768


def weight_rows(key, row_ids):
    base_key = jax.random.fold_in(key, 7)

    def single(vocab_id):
        return jax.random.truncated_normal(jax.random.fold_in(base_key, vocab_id), -6.0, 6.0, (D,), jnp.float32)
    return jax.vmap(single)(row_ids) * D ** (-0.5)


def draw_out_weight(key, part):
    blocks = jnp.arange(VOCAB, dtype=jnp.int32).reshape(256, VOCAB // 256)

    def one_block(block):
        return weight_rows(key, block).astype(jnp.bfloat16)
    values = lax.map(one_block, blocks)
    return values.reshape(VOCAB, D)


def draw_hidden(key, part):
    hidden_key = jax.random.fold_in(key, 3)
    drawn = jax.random.truncated_normal(jax.random.fold_in(hidden_key, 1), -6.0, 6.0, (ROWS, D), jnp.float32)
    return drawn.astype(jnp.bfloat16)


def draw_loss_mask(key, part):
    mask_key = jax.random.fold_in(key, 5)
    devices = ROWS // TOK_DEV
    random_bits = jax.random.randint(jax.random.fold_in(mask_key, 1), (devices, TOK_DEV), 0, 2)

    def one_order(sub_key):
        return jax.random.permutation(sub_key, TOK_DEV)
    orders = jax.vmap(one_order)(jax.random.split(jax.random.fold_in(mask_key, 2), devices))
    positions = jnp.arange(TOK_DEV, dtype=jnp.int32)
    forced = jnp.any(orders[:, :CAP, None] == positions[None, None, :], axis=1)
    return jnp.maximum(random_bits, forced.astype(jnp.int32)).reshape(ROWS).astype(jnp.int32)


def draw_kept_count(key, part):
    count_key = jax.random.fold_in(key, 9)
    devices = ROWS // TOK_DEV
    counts = jax.random.randint(jax.random.fold_in(count_key, 1), (devices,), 0, CAP + 1)
    full_at = jax.random.randint(jax.random.fold_in(count_key, 2), (), 0, devices)
    empty_at = (full_at + jax.random.randint(jax.random.fold_in(count_key, 3), (), 1, devices)) % devices
    device_ids = jnp.arange(devices)
    counts = jnp.where(device_ids == empty_at, 0, counts)
    return jnp.where(device_ids == full_at, CAP, counts).astype(jnp.int32)


def place_ends(result, stream_key, low, top_value):
    shape = result.shape
    place = [jax.random.randint(jax.random.fold_in(stream_key, axis), (), 0, shape[axis]) for axis in range(len(shape))]
    result = result.at[tuple(place)].set(low)
    longest = shape.index(max(shape))
    place[longest] = (place[longest] + 1) % shape[longest]
    return result.at[tuple(place)].set(top_value)


def ranked_wide(key, shape, count, skew):
    weights = [min(1 << octave, count + 1 - (1 << octave)) * (1 << 20) // math.isqrt((1 << octave) ** skew) + 1 for octave in range((count + 1).bit_length()) if 1 << octave <= count]
    width = 1 + sum(weights) // (1 << 30)
    listing = np.cumsum(np.array([max(1, weight // width) for weight in weights]))
    pick = jax.random.randint(jax.random.fold_in(key, 1), shape, 0, int(listing[len(weights) - 1]))
    start = jnp.left_shift(1, jnp.searchsorted(jnp.asarray(listing, jnp.int32), pick, side="right").astype(jnp.int32))
    rank = start - 1 + jax.random.randint(jax.random.fold_in(key, 4), shape, 0, 1 << 30) % jnp.minimum(start, count + 1 - start)
    return jax.random.permutation(jax.random.fold_in(key, 2), count)[rank].astype(jnp.int32)


def setup_inputs(seed: int = 0) -> dict:
    key_list = jax.random.split(jax.random.key(seed), 6)
    hidden = draw_hidden(jax.random.fold_in(key_list[5], 71), 0)
    out_weight = draw_out_weight(jax.random.fold_in(key_list[5], 71), 0)
    loss_mask = draw_loss_mask(jax.random.fold_in(key_list[5], 71), 0)
    targets = place_ends(ranked_wide(key_list[3], (ROWS,), VOCAB, 2), jax.random.fold_in(key_list[3], 3), 0, VOCAB - 1).astype(jnp.int32)
    kept_count = draw_kept_count(jax.random.fold_in(key_list[5], 71), 0)
    return {"hidden": hidden, "out_weight": out_weight, "loss_mask": loss_mask, "targets": targets, "kept_count": kept_count}


loss_scale = 128.0


def reference(hidden, out_weight, loss_mask, targets, kept_count):
    devices = kept_count.shape[0]
    per_device = hidden.shape[0] // devices
    mask_rows = loss_mask.reshape(devices, per_device)
    order_pos = jnp.cumsum(mask_rows, axis=1).astype(jnp.int32) - 1
    kept_row = (mask_rows == 1) & (order_pos < kept_count[:, None])
    slot_ids = jnp.arange(CAP, dtype=jnp.int32)
    slot_hits = kept_row[:, None, :] & (order_pos[:, None, :] == slot_ids[None, :, None])
    positions = jnp.arange(per_device, dtype=jnp.int32)
    local_row = jnp.sum(jnp.where(slot_hits, positions[None, None, :], 0), axis=2).astype(jnp.int32)
    filled = jnp.any(slot_hits, axis=2).reshape(-1)
    offsets = (jnp.arange(devices, dtype=jnp.int32) * per_device)[:, None]
    global_row = (local_row + offsets).reshape(-1).astype(jnp.int32)
    packed = jnp.where(filled[:, None], hidden[global_row], jnp.zeros((), hidden.dtype))
    packed_target = jnp.where(filled, targets[global_row], -1).astype(jnp.int32)
    logits = jnp.dot(packed, out_weight.T, preferred_element_type=jnp.float32)
    row_top = jnp.max(logits, axis=1)
    row_total = jnp.sum(jnp.exp(logits - row_top[:, None]), axis=1)
    log_total = row_top + jnp.log(row_total)
    vocab_ids = jnp.arange(logits.shape[1], dtype=jnp.int32)
    target_hit = vocab_ids[None, :] == packed_target[:, None]
    picked = jnp.sum(jnp.where(target_hit, logits, 0.0), axis=1)
    slot_loss = jnp.where(filled, log_total - picked, 0.0)
    probabilities = jnp.exp(logits - log_total[:, None])
    coefficient = jnp.where(filled[:, None], probabilities - target_hit.astype(logits.dtype), 0.0).astype(jnp.bfloat16)
    slot_grad = jnp.dot(coefficient, out_weight, preferred_element_type=jnp.float32) * loss_scale
    hidden_grad = jnp.zeros((hidden.shape[0], hidden.shape[1]), slot_grad.dtype).at[global_row].add(slot_grad)
    row_loss = jnp.zeros((hidden.shape[0],), slot_loss.dtype).at[global_row].add(slot_loss)
    return hidden_grad.astype(jnp.bfloat16), row_loss
```

```python
import jax
import jax.numpy as jnp
from jax import lax
from jax.sharding import Mesh, PartitionSpec as P

loss_scale = 128.0
send_scale = 32.0
send_type = jnp.float16


def device(x, y, c, z):
    return ((x * 4 + y) * 2 + c) * 8 + z


R4, R8 = range(4), range(8)
along_z = [[device(x, y, c, z) for z in R8] for x in R4 for y in R4 for c in (0, 1)]
along_x = [[[device(x, y, c, z) for x in R4] for y in R4 for z in R8] for c in (0, 1)]
along_y = [[[device(x, y, c, z) for y in R4] for x in R4 for z in R8] for c in (0, 1)]
inner = along_x[0] + along_y[1]
outer = along_y[0] + along_x[1]
same_core = [[device(x, y, c, z) for x in R4 for y in R4 for z in R8] for c in (0, 1)]
partner = [(device(x, y, c, z), device(x, y, 1 - c, z)) for x in R4 for y in R4 for c in (0, 1) for z in R8]


def exchange(value, groups):
    return lax.all_to_all(value, "d", 0, 0, axis_index_groups=groups)


def spread(value, groups):
    count = len(groups[0])
    return exchange(jnp.broadcast_to(value[None], (count,) + value.shape), groups)


def shards(hidden, out_weight, loss_mask, targets, kept_count):
    vocab_rows, width = out_weight.shape
    me = lax.axis_index("d")
    z, c, y, x = me % 8, (me // 8) % 2, (me // 16) % 4, me // 64
    other_weight = lax.ppermute(out_weight, "d", partner)

    positions = lax.broadcasted_iota(jnp.int32, loss_mask.shape, 0)
    first = jnp.min(jnp.where(loss_mask == 1, positions, loss_mask.shape[0]))
    kept_row = (positions == first) & (kept_count[0] > 0)
    code = jnp.sum(jnp.where(kept_row, targets + 1, 0))
    row = lax.dynamic_slice_in_dim(hidden, first, 1, 0)
    row = jnp.where(code > 0, row, jnp.zeros((), row.dtype))
    lane = lax.broadcasted_iota(jnp.int32, (1, 128), 1)
    digits = jnp.where(lane == 0, code % 256, jnp.where(lane == 1, (code // 256) % 256, jnp.where(lane == 2, code // 65536, 0)))
    packed = jnp.concatenate([row, digits.astype(row.dtype)], axis=1)

    rows = spread(packed, along_z).reshape(8, width + 128)
    rows = spread(rows, inner).reshape(32, width + 128)
    rows = spread(rows, outer).reshape(128, width + 128)
    gathered = rows[:, :width]
    digits = rows[:, width:width + 3].astype(jnp.int32)
    gathered_target = digits[:, 0] + 256 * digits[:, 1] + 65536 * digits[:, 2] - 1
    filled = gathered_target >= 0

    local = lax.broadcasted_iota(jnp.int32, (1, vocab_rows), 1)
    weights = (out_weight, other_weight)
    logits = [jnp.einsum("rd,vd->rv", gathered, w, preferred_element_type=jnp.float32) for w in weights]
    hits = [(local + base * vocab_rows) == gathered_target[:, None] for base in (me, me ^ 8)]
    top = jnp.maximum(jnp.max(logits[0], axis=1), jnp.max(logits[1], axis=1))
    total = sum(jnp.sum(jnp.exp(l - top[:, None]), axis=1) for l in logits)
    pick = sum(jnp.sum(jnp.where(h, l, 0.0), axis=1) for h, l in zip(hits, logits))
    stats = spread(jnp.stack([top, total, pick, pick]), same_core)
    row_top = jnp.max(stats[:, 0], axis=0)
    row_total = jnp.sum(stats[:, 1] * jnp.exp(stats[:, 0] - row_top[None]), axis=0)
    picked = jnp.sum(stats[:, 2], axis=0)
    log_total = row_top + jnp.log(row_total)
    slot_loss = jnp.where(filled, log_total - picked, 0.0)

    slot_grad = 0.0
    for l, h, w in zip(logits, hits, weights):
        coefficient = jnp.where(filled[:, None], jnp.exp(l - log_total[:, None]) - h.astype(jnp.float32), 0.0)
        slot_grad += jnp.dot(coefficient.astype(jnp.bfloat16), w, preferred_element_type=jnp.float32)
    part = (slot_grad * (loss_scale * send_scale)).astype(send_type).reshape(4, 32, width)
    part = jnp.sum(exchange(part, outer).astype(jnp.float32), axis=0)
    part = part.astype(send_type).reshape(4, 8, width)
    part = jnp.sum(exchange(part, inner).astype(jnp.float32), axis=0)
    part = part.astype(send_type).reshape(8, 1, width)
    own_grad = jnp.sum(exchange(part, along_z).astype(jnp.float32), axis=0) * (1.0 / send_scale)

    slot = jnp.where(c == 0, y * 4 + x, x * 4 + y) * 8 + z
    own_loss = lax.dynamic_slice_in_dim(slot_loss, slot, 1, 0)
    hidden_grad = jnp.where(kept_row[:, None], own_grad, 0.0).astype(jnp.bfloat16)
    row_loss = jnp.where(kept_row, own_loss, 0.0)
    return hidden_grad, row_loss


def solution(mesh):
    flat = Mesh(mesh.devices.reshape(-1), ("d",))
    rows = P("d", None)
    vector = P("d")
    return jax.shard_map(
        shards, mesh=flat, in_specs=(rows, rows, vector, vector, vector), out_specs=(rows, vector), check_vma=False
    )
```

```python
import functools

import jax
import jax.numpy as jnp
from jax import lax
from jax.experimental import pallas as pl
from jax.experimental.pallas import tpu as pltpu
from jax.sharding import Mesh, PartitionSpec as P

loss_scale = 128.0
send_scale = 32.0
send_type = jnp.float16
width = 8192
wide = width + 256
block = 1024
f32, bf16, i32 = jnp.float32, jnp.bfloat16, jnp.int32


def device(x, y, c, z):
    return ((x * 4 + y) * 2 + c) * 8 + z


R4, R8 = range(4), range(8)
places = [(x, y, c, z) for x in R4 for y in R4 for c in (0, 1) for z in R8]
along_z = [[device(x, y, c, z) for z in R8] for x in R4 for y in R4 for c in (0, 1)]
same_core = [[device(x, y, c, z) for x in R4 for y in R4 for z in R8] for c in (0, 1)]
partner = [(device(x, y, c, z), device(x, y, 1 - c, z)) for x, y, c, z in places]


def shift(value, outer, k):
    pairs = []
    for x, y, c, z in places:
        to = device(x, (y + k) % 4, c, z) if outer == (c == 0) else device((x + k) % 4, y, c, z)
        pairs.append((device(x, y, c, z), to))
    return lax.ppermute(value, "d", pairs)


def vmem(*args):
    return pl.BlockSpec(*args) if args else pl.BlockSpec(memory_space=pltpu.VMEM)


smem = pl.BlockSpec(memory_space=pltpu.SMEM)
anywhere = pl.BlockSpec(memory_space=pl.ANY)


def pack_kernel(count_ref, mask_ref, target_ref, hidden_ref, row_ref, kept_ref, slab, sem):
    lane = lax.broadcasted_iota(i32, (1, 128), 1)
    first = jnp.min(jnp.where(mask_ref[...] == 1, lane, 127).astype(f32)).astype(i32)
    copy = pltpu.make_async_copy(hidden_ref.at[pl.ds(pl.multiple_of(first // 8 * 8, 8), 8)], slab, sem)
    copy.start()
    kept = (lane == first) & (mask_ref[...] == 1) & (count_ref[0] > 0)
    kept_ref[...] = kept.astype(i32)
    code = jnp.sum(jnp.where(kept, target_ref[...] + 1, 0).astype(f32)).astype(i32)
    wide_lane = lax.broadcasted_iota(i32, (1, 256), 1)
    digits = jnp.where(wide_lane == 0, code % 256, 0) + jnp.where(wide_lane == 1, code // 256 % 256, 0)
    digits = digits + jnp.where(wide_lane == 2, code // 65536, 0)
    copy.wait()
    take = (lax.broadcasted_iota(i32, (8, width), 0) == first % 8) & (code > 0)
    row = jnp.sum(jnp.where(take, slab[...].astype(f32), 0.0), axis=0, keepdims=True)
    half = wide // 2
    low, high = row[:, :half], jnp.concatenate([row[:, half:], digits.astype(f32)], axis=1)
    both = jnp.where(lax.broadcasted_iota(i32, (2, half), 0) == 0, low, high).astype(bf16)
    row_ref[...] = jnp.broadcast_to(both[None], row_ref.shape)


def pack(count, mask, target, hidden):
    return pl.pallas_call(
        pack_kernel,
        in_specs=[smem, vmem(), vmem(), anywhere],
        out_specs=[vmem(), vmem()],
        out_shape=[jax.ShapeDtypeStruct((8, 2, wide // 2), bf16), jax.ShapeDtypeStruct((1, 128), i32)],
        scratch_shapes=[pltpu.VMEM((8, width), bf16), pltpu.SemaphoreType.DMA],
        name="pack",
    )(count, mask.reshape(1, 128), target.reshape(1, 128), hidden)


def by_rank(values, i, j):
    values = pltpu.roll(values, j * 32, 1)
    lane = lax.broadcasted_iota(i32, values.shape, 1)
    return jnp.where(lane % 32 >= i * 8, pltpu.roll(values, i * 8, 1), pltpu.roll(values, (i * 8 + 96) % 128, 1))


def by_arrival(values, i, j):
    lane = lax.broadcasted_iota(i32, values.shape, 1)
    back, around = pltpu.roll(values, (128 - i * 8) % 128, 1), pltpu.roll(values, 32 - i * 8, 1)
    return pltpu.roll(jnp.where(lane % 32 < 32 - i * 8, back, around), (128 - j * 32) % 128, 1)


def logits_kernel(vocab_rows, place_ref, r0, r1, r2, r3, digits_ref, w_ref, v_ref, own_ref, other_ref, stats_ref):
    step = pl.program_id(0)
    rows = jnp.concatenate([r0[...], r1[...], r2[...], r3[...]], axis=0)

    @pl.when(step == 0)
    def _():
        own_ref[...] = jnp.zeros_like(own_ref)
        other_ref[...] = jnp.zeros_like(other_ref)

    for out, weight in ((own_ref, w_ref), (other_ref, v_ref)):
        out[...] += lax.dot_general(weight[...], rows, (((1,), (1,)), ((), ())), preferred_element_type=f32)

    @pl.when(step == pl.num_programs(0) - 1)
    def _():
        i, j, me = place_ref[0], place_ref[1], place_ref[2]
        digits = digits_ref[...]
        target = digits[0:1] + 256 * digits[1:2] + 65536 * digits[2:3] - 1
        top = jnp.maximum(jnp.max(own_ref[...], axis=0, keepdims=True), jnp.max(other_ref[...], axis=0, keepdims=True))
        total, pick = 0.0, 0.0
        for out, base in ((own_ref, me), (other_ref, me ^ 8)):
            ids = lax.broadcasted_iota(i32, (vocab_rows, 128), 0) + base * vocab_rows
            total += jnp.sum(jnp.exp(out[...] - top), axis=0, keepdims=True)
            pick += jnp.sum(jnp.where(ids == target, out[...], 0.0), axis=0, keepdims=True)
        row = lax.broadcasted_iota(i32, (4, 128), 0)
        stats = jnp.where(row == 0, top, jnp.where(row == 1, total, jnp.where(row == 2, pick, target.astype(f32))))
        stats_ref[...] = jnp.broadcast_to(by_rank(stats, i, j)[None], stats_ref.shape)


def logits_call(place, rows, digits, own, other):
    vocab_rows = own.shape[0]
    part = pl.BlockSpec((32, block), lambda k: (0, k))
    weight = pl.BlockSpec((vocab_rows, block), lambda k: (0, k))
    logits = pl.BlockSpec((vocab_rows, 128), lambda k: (0, 0))
    return pl.pallas_call(
        functools.partial(logits_kernel, vocab_rows),
        grid=(width // block,),
        in_specs=[smem, part, part, part, part, pl.BlockSpec((4, 128), lambda k: (0, 0)), weight, weight],
        out_specs=[logits, logits, pl.BlockSpec((128, 4, 128), lambda k: (0, 0, 0))],
        out_shape=[jax.ShapeDtypeStruct((vocab_rows, 128), f32)] * 2 + [jax.ShapeDtypeStruct((128, 4, 128), f32)],
        name="logits",
    )(place, *rows, digits, own, other)


def grad_kernel(vocab_rows, place_ref, stats_ref, own_ref, other_ref, w_ref, v_ref, g0, g1, g2, g3, loss_ref, coefs):
    step = pl.program_id(0)

    @pl.when(step == 0)
    def _():
        i, j, me = place_ref[0], place_ref[1], place_ref[2]
        top = jnp.max(stats_ref[:, 0, :], axis=0, keepdims=True)
        total = jnp.sum(stats_ref[:, 1, :] * jnp.exp(stats_ref[:, 0, :] - top), axis=0, keepdims=True)
        picked = jnp.sum(stats_ref[:, 2, :], axis=0, keepdims=True)
        target = stats_ref[0, 3:4, :]
        log_total = top + jnp.log(total)
        loss_ref[...] = jnp.where(target >= 0, log_total - picked, 0.0)
        row = lax.broadcasted_iota(i32, (8, 128), 0)
        both = by_arrival(jnp.where(row == 0, log_total, target), i, j)
        log_total, target = both[0:1], both[1:2].astype(i32)
        for slot, (out, base) in enumerate(((own_ref, me), (other_ref, me ^ 8))):
            ids = lax.broadcasted_iota(i32, (vocab_rows, 128), 0) + base * vocab_rows
            hit = (ids == target).astype(f32)
            coefs[slot] = jnp.where(target >= 0, jnp.exp(out[...] - log_total) - hit, 0.0).T.astype(bf16)

    grad = jnp.dot(coefs[0], w_ref[...], preferred_element_type=f32)
    grad += jnp.dot(coefs[1], v_ref[...], preferred_element_type=f32)
    grad = grad * (loss_scale * send_scale)
    for k, out in enumerate((g0, g1, g2, g3)):
        out[...] = grad[k * 32:(k + 1) * 32].astype(out.dtype)


def grad_call(place, stats, logits, own, other, out_type):
    vocab_rows = own.shape[0]
    part = pl.BlockSpec((32, block), lambda k: (0, k))
    weight = pl.BlockSpec((vocab_rows, block), lambda k: (0, k))
    held = pl.BlockSpec((vocab_rows, 128), lambda k: (0, 0))
    return pl.pallas_call(
        functools.partial(grad_kernel, vocab_rows),
        grid=(width // block,),
        in_specs=[smem, pl.BlockSpec((128, 4, 128), lambda k: (0, 0, 0)), held, held, weight, weight],
        out_specs=[part] * 4 + [pl.BlockSpec((1, 128), lambda k: (0, 0))],
        out_shape=[jax.ShapeDtypeStruct((32, width), out_type)] * 4 + [jax.ShapeDtypeStruct((1, 128), f32)],
        scratch_shapes=[pltpu.VMEM((2, 128, vocab_rows), bf16)],
        name="grad",
    )(place, stats, *logits, own, other)


def exchange(value, groups):
    return lax.all_to_all(value, "d", 0, 0, axis_index_groups=groups)


def gather4(value, outer):
    far, back, on = shift(value, outer, 2), shift(value, outer, 1), shift(value, outer, 3)
    return [value, on, far, back]


def reduce4(blocks, outer):
    far, on, back = shift(blocks[2], outer, 2), shift(blocks[1], outer, 1), shift(blocks[3], outer, 3)
    return (blocks[0].astype(f32) + on.astype(f32)) + (far.astype(f32) + back.astype(f32))


def shards(hidden, out_weight, loss_mask, targets, kept_count):
    me = lax.axis_index("d")
    z, c, y, x = me % 8, (me // 8) % 2, (me // 16) % 4, me // 64
    i, j = jnp.where(c == 0, x, y), jnp.where(c == 0, y, x)
    place = jnp.stack([i, j, me])
    other_weight = lax.ppermute(out_weight, "d", partner)

    packed, kept = pack(kept_count, loss_mask, targets, hidden)
    rows = exchange(packed, along_z).reshape(8, wide)
    rows = jnp.concatenate(gather4(rows, False), axis=0)
    rows = gather4(rows, True)
    digits = jnp.concatenate([r[:, width:width + 4] for r in rows], axis=0).T.astype(i32)
    *logits, stats = logits_call(place, rows, digits, out_weight, other_weight)
    stats = exchange(stats, same_core)
    *parts, loss = grad_call(place, stats, logits, out_weight, other_weight, OUT)
    part = reduce4([p.astype(send_type) for p in parts], True)
    part = part.astype(send_type)
    part = reduce4([part[k * 8:(k + 1) * 8] for k in R4], False)
    part = exchange(part.astype(send_type).reshape(8, 1, width), along_z)
    own_grad = jnp.sum(part.astype(f32), axis=0) * (1.0 / send_scale)

    own_loss = lax.dynamic_slice_in_dim(loss[0], (j * 4 + i) * 8 + z, 1, 0)
    kept_row = kept[0] > 0
    hidden_grad = jnp.where(kept_row[:, None], own_grad, 0.0).astype(bf16)
    row_loss = jnp.where(kept_row, own_loss, 0.0)
    return hidden_grad, row_loss


OUT = jnp.float32


def solution(mesh):
    flat = Mesh(mesh.devices.reshape(-1), ("d",))
    rows = P("d", None)
    vector = P("d")
    return jax.shard_map(
        shards, mesh=flat, in_specs=(rows, rows, vector, vector, vector), out_specs=(rows, vector), check_vma=False
    )
```

```python
import functools

import jax
import jax.numpy as jnp
from jax import lax
from jax.experimental import pallas as pl
from jax.experimental.pallas import tpu as pltpu
from jax.sharding import Mesh, PartitionSpec as P

loss_scale = 128.0
send_scale = 32.0
send_type = jnp.float16
width = 8192
wide = width + 256


def spans(sizes):
    return [(sum(sizes[:k]), size) for k, size in enumerate(sizes)]


logit_chunks = spans([1024, 1024, 2048, 2048, 2048])
grad_chunks = spans([1024, 2048, 2048, 2048, 1024])
f32, bf16, i32 = jnp.float32, jnp.bfloat16, jnp.int32


def device(x, y, c, z):
    return ((x * 4 + y) * 2 + c) * 8 + z


R4, R8 = range(4), range(8)
places = [(x, y, c, z) for x in R4 for y in R4 for c in (0, 1) for z in R8]
along_z = [[device(x, y, c, z) for z in R8] for x in R4 for y in R4 for c in (0, 1)]
same_core = [[device(x, y, c, z) for x in R4 for y in R4 for z in R8] for c in (0, 1)]
partner = [(device(x, y, c, z), device(x, y, 1 - c, z)) for x, y, c, z in places]


def shift(value, outer, k):
    pairs = []
    for x, y, c, z in places:
        to = device(x, (y + k) % 4, c, z) if outer == (c == 0) else device((x + k) % 4, y, c, z)
        pairs.append((device(x, y, c, z), to))
    return lax.ppermute(value, "d", pairs)


def vmem(*args):
    return pl.BlockSpec(*args) if args else pl.BlockSpec(memory_space=pltpu.VMEM)


smem = pl.BlockSpec(memory_space=pltpu.SMEM)
anywhere = pl.BlockSpec(memory_space=pl.ANY)


def pack_kernel(count_ref, mask_ref, target_ref, hidden_ref, row_ref, kept_ref, slab, sem):
    lane = lax.broadcasted_iota(i32, (1, 128), 1)
    first = jnp.min(jnp.where(mask_ref[...] == 1, lane, 127).astype(f32)).astype(i32)
    copy = pltpu.make_async_copy(hidden_ref.at[pl.ds(pl.multiple_of(first // 8 * 8, 8), 8)], slab, sem)
    copy.start()
    kept = (lane == first) & (mask_ref[...] == 1) & (count_ref[0] > 0)
    kept_ref[...] = kept.astype(i32)
    code = jnp.sum(jnp.where(kept, target_ref[...] + 1, 0).astype(f32)).astype(i32)
    wide_lane = lax.broadcasted_iota(i32, (1, 256), 1)
    digits = jnp.where(wide_lane == 0, code % 256, 0) + jnp.where(wide_lane == 1, code // 256 % 256, 0)
    digits = digits + jnp.where(wide_lane == 2, code // 65536, 0)
    copy.wait()
    take = (lax.broadcasted_iota(i32, (8, width), 0) == first % 8) & (code > 0)
    row = jnp.sum(jnp.where(take, slab[...].astype(f32), 0.0), axis=0, keepdims=True)
    half = wide // 2
    low, high = row[:, :half], jnp.concatenate([row[:, half:], digits.astype(f32)], axis=1)
    both = jnp.where(lax.broadcasted_iota(i32, (2, half), 0) == 0, low, high).astype(bf16)
    row_ref[...] = jnp.broadcast_to(both[None], row_ref.shape)


def pack(count, mask, target, hidden):
    return pl.pallas_call(
        pack_kernel,
        in_specs=[smem, vmem(), vmem(), anywhere],
        out_specs=[vmem(), vmem()],
        out_shape=[jax.ShapeDtypeStruct((8, 2, wide // 2), bf16), jax.ShapeDtypeStruct((1, 128), i32)],
        scratch_shapes=[pltpu.VMEM((8, width), bf16), pltpu.SemaphoreType.DMA],
        name="pack",
    )(count, mask.reshape(1, 128), target.reshape(1, 128), hidden)


def by_rank(values, i, j):
    values = pltpu.roll(values, j * 32, 1)
    lane = lax.broadcasted_iota(i32, values.shape, 1)
    return jnp.where(lane % 32 >= i * 8, pltpu.roll(values, i * 8, 1), pltpu.roll(values, (i * 8 + 96) % 128, 1))


def by_arrival(values, i, j):
    lane = lax.broadcasted_iota(i32, values.shape, 1)
    back, around = pltpu.roll(values, (128 - i * 8) % 128, 1), pltpu.roll(values, 32 - i * 8, 1)
    return pltpu.roll(jnp.where(lane % 32 < 32 - i * 8, back, around), (128 - j * 32) % 128, 1)


def fetch(pairs, sems):
    copies = [[pltpu.make_async_copy(a, b, sems.at[k, n]) for n, (a, b) in enumerate(p)] for k, p in enumerate(pairs)]
    for chunk in copies:
        for copy in chunk:
            copy.start()
    return copies


def logits_kernel(vocab_rows, place_ref, digits_ref, r0, r1, r2, r3, w_ref, v_ref, own_ref, other_ref, stats_ref, rows, weights, sems):
    pairs = []
    for start, size in logit_chunks:
        cols = pl.ds(start, size)
        pair = [(w_ref.at[:, cols], weights.at[0, :, cols]), (v_ref.at[:, cols], weights.at[1, :, cols])]
        pair += [(r.at[:, cols], rows.at[pl.ds(k * 32, 32), cols]) for k, r in enumerate((r0, r1, r2, r3))]
        pairs.append(pair)
    copies = fetch(pairs, sems)
    for k, (start, size) in enumerate(logit_chunks):
        for copy in copies[k]:
            copy.wait()
        cols = pl.ds(start, size)
        for slot, out in enumerate((own_ref, other_ref)):
            part = lax.dot_general(
                weights[slot, :, cols], rows[:, cols], (((1,), (1,)), ((), ())), preferred_element_type=f32
            )
            out[...] = part if k == 0 else out[...] + part

    i, j, me = place_ref[0], place_ref[1], place_ref[2]
    target = digits_ref[0:1] + 256 * digits_ref[1:2] + 65536 * digits_ref[2:3] - 1
    top = jnp.maximum(jnp.max(own_ref[...], axis=0, keepdims=True), jnp.max(other_ref[...], axis=0, keepdims=True))
    total, pick = 0.0, 0.0
    for out, base in ((own_ref, me), (other_ref, me ^ 8)):
        ids = lax.broadcasted_iota(i32, (vocab_rows, 128), 0) + base * vocab_rows
        total += jnp.sum(jnp.exp(out[...] - top), axis=0, keepdims=True)
        pick += jnp.sum(jnp.where(ids == target, out[...], 0.0), axis=0, keepdims=True)
    row = lax.broadcasted_iota(i32, (8, 128), 0)
    stats = jnp.where(row == 0, top + jnp.log(total), pick)
    stats_ref[...] = jnp.broadcast_to(by_rank(stats, i, j)[None, :2], stats_ref.shape)


def logits_call(place, digits, rows, own, other):
    vocab_rows = own.shape[0]
    return pl.pallas_call(
        functools.partial(logits_kernel, vocab_rows),
        in_specs=[smem, vmem()] + [anywhere] * 6,
        out_specs=[vmem()] * 3,
        out_shape=[jax.ShapeDtypeStruct((vocab_rows, 128), f32)] * 2 + [jax.ShapeDtypeStruct((128, 2, 128), f32)],
        scratch_shapes=[
            pltpu.VMEM((128, width), bf16),
            pltpu.VMEM((2, vocab_rows, width), bf16),
            pltpu.SemaphoreType.DMA((len(logit_chunks), 6)),
        ],
        name="logits",
    )(place, digits, *rows, own, other)


def grad_kernel(
    vocab_rows, place_ref, digits_ref, stats_ref, own_ref, other_ref, w_ref, v_ref, g0, g1, g2, g3, loss_ref, coefs, weights, grads, sems, sent
):
    pairs = []
    for start, size in grad_chunks:
        cols = pl.ds(start, size)
        pairs.append([(w_ref.at[:, cols], weights.at[0, :, cols]), (v_ref.at[:, cols], weights.at[1, :, cols])])
    copies = fetch(pairs, sems)

    i, j, me = place_ref[0], place_ref[1], place_ref[2]
    lse = stats_ref[:, 0, :]
    top = jnp.max(lse, axis=0, keepdims=True)
    log_total = top + jnp.log(jnp.sum(jnp.exp(lse - top), axis=0, keepdims=True))
    picked = jnp.sum(stats_ref[:, 1, :], axis=0, keepdims=True)
    target = digits_ref[0:1] + 256 * digits_ref[1:2] + 65536 * digits_ref[2:3] - 1
    loss_ref[...] = log_total - picked
    log_total = by_arrival(jnp.broadcast_to(log_total, (8, 128)), i, j)[0:1]
    for slot, (out, base) in enumerate(((own_ref, me), (other_ref, me ^ 8))):
        ids = lax.broadcasted_iota(i32, (vocab_rows, 128), 0) + base * vocab_rows
        hit = (ids == target).astype(f32)
        coefs[slot] = jnp.where(target >= 0, jnp.exp(out[...] - log_total) - hit, 0.0).T.astype(bf16)

    out_copies = []
    for k, (start, size) in enumerate(grad_chunks):
        for copy in copies[k]:
            copy.wait()
        cols = pl.ds(start, size)
        grad = jnp.dot(coefs[0], weights[0, :, cols], preferred_element_type=f32)
        grad += jnp.dot(coefs[1], weights[1, :, cols], preferred_element_type=f32)
        grads[:, cols] = grad * (loss_scale * send_scale)
        for n, out in enumerate((g0, g1, g2, g3)):
            copy = pltpu.make_async_copy(grads.at[pl.ds(n * 32, 32), cols], out.at[:, cols], sent.at[k, n])
            copy.start()
            out_copies.append(copy)
    for copy in out_copies:
        copy.wait()


def grad_call(place, digits, stats, logits, own, other):
    vocab_rows = own.shape[0]
    return pl.pallas_call(
        functools.partial(grad_kernel, vocab_rows),
        in_specs=[smem] + [vmem()] * 4 + [anywhere] * 2,
        out_specs=[anywhere] * 4 + [vmem()],
        out_shape=[jax.ShapeDtypeStruct((32, width), f32)] * 4 + [jax.ShapeDtypeStruct((1, 128), f32)],
        scratch_shapes=[
            pltpu.VMEM((2, 128, vocab_rows), bf16),
            pltpu.VMEM((2, vocab_rows, width), bf16),
            pltpu.VMEM((128, width), f32),
            pltpu.SemaphoreType.DMA((len(grad_chunks), 2)),
            pltpu.SemaphoreType.DMA((len(grad_chunks), 4)),
        ],
        name="grad",
    )(place, digits, stats, *logits, own, other)


def exchange(value, groups):
    return lax.all_to_all(value, "d", 0, 0, axis_index_groups=groups)


def gather4(value, outer):
    far, back, on = shift(value, outer, 2), shift(value, outer, 1), shift(value, outer, 3)
    return [value, on, far, back]


def reduce4(blocks, outer):
    far, on, back = shift(blocks[2], outer, 2), shift(blocks[1], outer, 1), shift(blocks[3], outer, 3)
    return (blocks[0].astype(f32) + on.astype(f32)) + (far.astype(f32) + back.astype(f32))


def shards(hidden, out_weight, loss_mask, targets, kept_count):
    me = lax.axis_index("d")
    z, c, y, x = me % 8, (me // 8) % 2, (me // 16) % 4, me // 64
    i, j = jnp.where(c == 0, x, y), jnp.where(c == 0, y, x)
    place = jnp.stack([i, j, me])
    other_weight = lax.ppermute(out_weight, "d", partner)

    packed, kept = pack(kept_count, loss_mask, targets, hidden)
    rows = exchange(packed, along_z).reshape(8, wide)
    rows = jnp.concatenate(gather4(rows, False), axis=0)
    rows = gather4(rows, True)
    digits = jnp.concatenate([r[:, width:width + 4] for r in rows], axis=0).T.astype(i32)
    *logits, stats = logits_call(place, digits, rows, out_weight, other_weight)
    stats = exchange(stats, same_core)
    *parts, loss = grad_call(place, digits, stats, logits, out_weight, other_weight)
    part = reduce4([p.astype(send_type) for p in parts], True)
    part = part.astype(send_type)
    part = reduce4([part[k * 8:(k + 1) * 8] for k in R4], False)
    part = exchange(part.astype(send_type).reshape(8, width // 128, 128), along_z)
    own_grad = (jnp.sum(part.astype(f32), axis=0) * (1.0 / send_scale)).reshape(1, width)

    own_loss = lax.dynamic_slice_in_dim(loss[0], (j * 4 + i) * 8 + z, 1, 0)
    kept_row = kept[0] > 0
    hidden_grad = jnp.where(kept_row[:, None], own_grad, 0.0).astype(bf16)
    row_loss = jnp.where(kept_row, own_loss, 0.0)
    return hidden_grad, row_loss


def solution(mesh):
    flat = Mesh(mesh.devices.reshape(-1), ("d",))
    rows = P("d", None)
    vector = P("d")
    return jax.shard_map(
        shards, mesh=flat, in_specs=(rows, rows, vector, vector, vector), out_specs=(rows, vector), check_vma=False
    )
```

```python
import functools

import jax
import jax.numpy as jnp
from jax import lax
from jax.experimental import pallas as pl
from jax.experimental.pallas import tpu as pltpu
from jax.sharding import Mesh, PartitionSpec as P


loss_scale = 128.0
send_scale = 32.0
send_type = jnp.float16
width = 8192
wide = width + 256


def spans(sizes):
    return [(sum(sizes[:k]), size) for k, size in enumerate(sizes)]


middle = width // 2
f32, bf16, i32 = jnp.float32, jnp.bfloat16, jnp.int32


def device(x, y, c, z):
    return ((x * 4 + y) * 2 + c) * 8 + z


R4, R8 = range(4), range(8)
places = [(x, y, c, z) for x in R4 for y in R4 for c in (0, 1) for z in R8]
along_z = [[device(x, y, c, z) for z in R8] for x in R4 for y in R4 for c in (0, 1)]
same_core = [[device(x, y, c, z) for x in R4 for y in R4 for z in R8] for c in (0, 1)]
partner = [(device(x, y, c, z), device(x, y, 1 - c, z)) for x, y, c, z in places]


def shift(value, outer, k):
    pairs = []
    for x, y, c, z in places:
        to = device(x, (y + k) % 4, c, z) if outer == (c == 0) else device((x + k) % 4, y, c, z)
        pairs.append((device(x, y, c, z), to))
    return lax.ppermute(value, "d", pairs)


def vmem(*args):
    return pl.BlockSpec(*args) if args else pl.BlockSpec(memory_space=pltpu.VMEM)


smem = pl.BlockSpec(memory_space=pltpu.SMEM)
anywhere = pl.BlockSpec(memory_space=pl.ANY)


def pack_kernel(count_ref, mask_ref, target_ref, hidden_ref, row_ref, kept_ref, slab, sem):
    lane = lax.broadcasted_iota(i32, (1, 128), 1)
    first = jnp.min(jnp.where(mask_ref[...] == 1, lane, 127).astype(f32)).astype(i32)
    copy = pltpu.make_async_copy(hidden_ref.at[pl.ds(pl.multiple_of(first // 8 * 8, 8), 8)], slab, sem)
    copy.start()
    kept = (lane == first) & (mask_ref[...] == 1) & (count_ref[0] > 0)
    kept_ref[...] = kept.astype(i32)
    code = jnp.sum(jnp.where(kept, target_ref[...] + 1, 0).astype(f32)).astype(i32)
    wide_lane = lax.broadcasted_iota(i32, (1, 256), 1)
    digits = jnp.where(wide_lane == 0, code % 256, 0) + jnp.where(wide_lane == 1, code // 256 % 256, 0)
    digits = digits + jnp.where(wide_lane == 2, code // 65536, 0)
    copy.wait()
    take = (lax.broadcasted_iota(i32, (8, width), 0) == first % 8) & (code > 0)
    row = jnp.sum(jnp.where(take, slab[...].astype(f32), 0.0), axis=0, keepdims=True)
    half = wide // 2
    low, high = row[:, :half], jnp.concatenate([row[:, half:], digits.astype(f32)], axis=1)
    both = jnp.where(lax.broadcasted_iota(i32, (2, half), 0) == 0, low, high).astype(bf16)
    row_ref[...] = jnp.broadcast_to(both[None], row_ref.shape)


def pack(count, mask, target, hidden):
    return pl.pallas_call(
        pack_kernel,
        in_specs=[smem, vmem(), vmem(), anywhere],
        out_specs=[vmem(), vmem()],
        out_shape=[jax.ShapeDtypeStruct((8, 2, wide // 2), bf16), jax.ShapeDtypeStruct((1, 128), i32)],
        scratch_shapes=[pltpu.VMEM((8, width), bf16), pltpu.SemaphoreType.DMA],
        name="pack",
    )(count, mask.reshape(1, 128), target.reshape(1, 128), hidden)


def by_rank(values, i, j):
    values = pltpu.roll(values, j * 32, 1)
    lane = lax.broadcasted_iota(i32, values.shape, 1)
    return jnp.where(lane % 32 >= i * 8, pltpu.roll(values, i * 8, 1), pltpu.roll(values, (i * 8 + 96) % 128, 1))


def by_arrival(values, i, j):
    lane = lax.broadcasted_iota(i32, values.shape, 1)
    back, around = pltpu.roll(values, (128 - i * 8) % 128, 1), pltpu.roll(values, 32 - i * 8, 1)
    return pltpu.roll(jnp.where(lane % 32 < 32 - i * 8, back, around), (128 - j * 32) % 128, 1)


def fetch(pairs, sems):
    copies = [[pltpu.make_async_copy(a, b, sems.at[k, n]) for n, (a, b) in enumerate(p)] for k, p in enumerate(pairs)]
    for chunk in copies:
        for copy in chunk:
            copy.start()
    return copies


def weight_copies(chunks, start, w_ref, v_ref, weights):
    pairs = []
    for at, size in chunks:
        source, held = pl.ds(start + at, size), pl.ds(at, size)
        pairs.append([(w_ref.at[:, source], weights.at[0, :, held]), (v_ref.at[:, source], weights.at[1, :, held])])
    return pairs


def logits_kernel(half, vocab_rows, *refs):
    if half == 0:
        r0, r1, r2, r3, w_ref, v_ref, own_ref, other_ref, rows, weights, sems = refs
        chunks = spans([1024, 1024, 2048])
    else:
        place_ref, own_in, other_in, r0, r1, r2, r3, w_ref, v_ref = refs[:9]
        own_ref, other_ref, stats_ref, target_ref, rows, weights, sems = refs[9:]
        chunks = spans([2048, 1024, 1024])
    pairs = weight_copies(chunks, half * middle, w_ref, v_ref, weights)
    for pair, (at, size) in zip(pairs, chunks):
        size += (wide - width) * (half == 1 and at + size == middle)
        cols = pl.ds(at, size)
        pair += [(r.at[:, cols], rows.at[pl.ds(k * 32, 32), cols]) for k, r in enumerate((r0, r1, r2, r3))]
    copies = fetch(pairs, sems)
    for k, (at, size) in enumerate(chunks):
        for copy in copies[k]:
            copy.wait()
        cols = pl.ds(at, size)
        for slot, out in enumerate((own_ref, other_ref)):
            part = lax.dot_general(
                weights[slot, :, cols], rows[:, cols], (((1,), (1,)), ((), ())), preferred_element_type=f32
            )
            if k:
                part = out[...] + part
            elif half:
                part = (own_in, other_in)[slot][...] + part
            out[...] = part
    if half == 0:
        return

    i, j, me = place_ref[0], place_ref[1], place_ref[2]
    digits = rows[:, pl.ds(middle, 128)].astype(f32).T
    target = (digits[0:1] + 256 * digits[1:2] + 65536 * digits[2:3]).astype(i32) - 1
    top = jnp.maximum(jnp.max(own_ref[...], axis=0, keepdims=True), jnp.max(other_ref[...], axis=0, keepdims=True))
    total, pick = 0.0, 0.0
    for out, base in ((own_ref, me), (other_ref, me ^ 8)):
        ids = lax.broadcasted_iota(i32, (vocab_rows, 128), 0) + base * vocab_rows
        total += jnp.sum(jnp.exp(out[...] - top), axis=0, keepdims=True)
        pick += jnp.sum(jnp.where(ids == target, out[...], 0.0), axis=0, keepdims=True)
    row = lax.broadcasted_iota(i32, (8, 128), 0)
    stats = jnp.where(row == 0, top + jnp.log(total), pick)
    stats_ref[...] = jnp.broadcast_to(by_rank(stats, i, j)[None, :2], stats_ref.shape)
    target_ref[...] = target


def logits_call(half, place, partial, rows, own, other):
    vocab_rows = own.shape[0]
    partial_shape = [jax.ShapeDtypeStruct((vocab_rows, 128), f32)] * 2
    stats_shape = [jax.ShapeDtypeStruct((128, 2, 128), f32), jax.ShapeDtypeStruct((1, 128), i32)]
    return pl.pallas_call(
        functools.partial(logits_kernel, half, vocab_rows),
        in_specs=([smem] + [vmem()] * 2) * half + [anywhere] * 6,
        out_specs=[vmem()] * (4 if half else 2),
        out_shape=partial_shape + stats_shape * half,
        scratch_shapes=[
            pltpu.VMEM((128, middle + (wide - width) * half), bf16),
            pltpu.VMEM((2, vocab_rows, middle), bf16),
            pltpu.SemaphoreType.DMA((3, 6)),
        ],
    )(*(([place] + list(partial)) if half else []), *rows, own, other)


def grad_kernel(half, vocab_rows, *refs):
    if half == 0:
        place_ref, target_ref, stats_ref, own_ref, other_ref, w_ref, v_ref = refs[:7]
        g0, g1, g2, g3, loss_ref, coefs, weights, grads, sems, sent = refs[7:]
        chunks = spans([1024, 2048, 1024])
    else:
        coefs, w_ref, v_ref, g0, g1, g2, g3, weights, grads, sems, sent = refs
        chunks = spans([1024, 2048, 1024])
    copies = fetch(weight_copies(chunks, half * middle, w_ref, v_ref, weights), sems)

    if half == 0:
        i, j, me = place_ref[0], place_ref[1], place_ref[2]
        lse = stats_ref[:, 0, :]
        top = jnp.max(lse, axis=0, keepdims=True)
        log_total = top + jnp.log(jnp.sum(jnp.exp(lse - top), axis=0, keepdims=True))
        picked = jnp.sum(stats_ref[:, 1, :], axis=0, keepdims=True)
        target = target_ref[...]
        loss_ref[...] = log_total - picked
        log_total = by_arrival(jnp.broadcast_to(log_total, (8, 128)), i, j)[0:1]
        for slot, (out, base) in enumerate(((own_ref, me), (other_ref, me ^ 8))):
            ids = lax.broadcasted_iota(i32, (vocab_rows, 128), 0) + base * vocab_rows
            hit = (ids == target).astype(f32)
            coefs[slot] = jnp.where(target >= 0, jnp.exp(out[...] - log_total) - hit, 0.0).T.astype(bf16)

    out_copies = []
    for k, (at, size) in enumerate(chunks):
        for copy in copies[k]:
            copy.wait()
        cols = pl.ds(at, size)
        grad = jnp.dot(coefs[0], weights[0, :, cols], preferred_element_type=f32)
        grad += jnp.dot(coefs[1], weights[1, :, cols], preferred_element_type=f32)
        grads[:, cols] = grad * (loss_scale * send_scale)
        for n, out in enumerate((g0, g1, g2, g3)):
            copy = pltpu.make_async_copy(grads.at[pl.ds(n * 32, 32), cols], out.at[:, cols], sent.at[k, n])
            copy.start()
            out_copies.append(copy)
    for copy in out_copies:
        copy.wait()


def grad_call(half, args, own, other):
    vocab_rows = own.shape[0]
    shapes = [jax.ShapeDtypeStruct((1, 128), f32), jax.ShapeDtypeStruct((2, 128, vocab_rows), bf16)]
    return pl.pallas_call(
        functools.partial(grad_kernel, half, vocab_rows),
        in_specs=([vmem()] if half else [smem] + [vmem()] * 4) + [anywhere] * 2,
        out_specs=[anywhere] * 4 + [vmem()] * (0 if half else 2),
        out_shape=[jax.ShapeDtypeStruct((32, middle), f32)] * 4 + ([] if half else shapes),
        scratch_shapes=[
            pltpu.VMEM((2, vocab_rows, middle), bf16),
            pltpu.VMEM((128, middle), f32),
            pltpu.SemaphoreType.DMA((3, 2)),
            pltpu.SemaphoreType.DMA((3, 4)),
        ],
    )(*args, own, other)


def exchange(value, groups):
    return lax.all_to_all(value, "d", 0, 0, axis_index_groups=groups)


def gather4(value, outer):
    far, back, on = shift(value, outer, 2), shift(value, outer, 1), shift(value, outer, 3)
    return [value, on, far, back]


def reduce4(blocks, outer):
    far, on, back = shift(blocks[2], outer, 2), shift(blocks[1], outer, 1), shift(blocks[3], outer, 3)
    return (blocks[0].astype(f32) + on.astype(f32)) + (far.astype(f32) + back.astype(f32))


def shards(hidden, out_weight, loss_mask, targets, kept_count):
    me = lax.axis_index("d")
    z, c, y, x = me % 8, (me // 8) % 2, (me // 16) % 4, me // 64
    i, j = jnp.where(c == 0, x, y), jnp.where(c == 0, y, x)
    place = jnp.stack([i, j, me])
    other_weight = lax.ppermute(out_weight, "d", partner)

    packed, kept = pack(kept_count, loss_mask, targets, hidden)
    rows = gather4(exchange(packed, along_z).reshape(8, wide), False)
    halves = [jnp.concatenate([r[:, a:b] for r in rows], axis=0) for a, b in ((0, middle), (middle, wide))]
    first = gather4(halves[0], True)
    halves = [first, gather4(halves[1], True)]
    partial = logits_call(0, place, None, halves[0], out_weight, other_weight)
    *logits, stats, target = logits_call(1, place, partial, halves[1], out_weight, other_weight)
    stats = exchange(stats, same_core)
    *first, loss, coefs = grad_call(0, (place, target, stats, *logits), out_weight, other_weight)
    second = grad_call(1, (coefs,), out_weight, other_weight)
    parts = [reduce4([p.astype(send_type) for p in blocks], True) for blocks in (first, second)]
    part = jnp.concatenate(parts, axis=1).astype(send_type)
    part = reduce4([part[k * 8:(k + 1) * 8] for k in R4], False)
    part = exchange(part.astype(send_type).reshape(8, width // 128, 128), along_z)
    own_grad = (jnp.sum(part.astype(f32), axis=0) * (1.0 / send_scale)).reshape(1, width)

    own_loss = lax.dynamic_slice_in_dim(loss[0], (j * 4 + i) * 8 + z, 1, 0)
    kept_row = kept[0] > 0
    hidden_grad = jnp.where(kept_row[:, None], own_grad, 0.0).astype(bf16)
    row_loss = jnp.where(kept_row, own_loss, 0.0)
    return hidden_grad, row_loss


def solution(mesh):
    flat = Mesh(mesh.devices.reshape(-1), ("d",))
    rows = P("d", None)
    vector = P("d")
    return jax.shard_map(
        shards, mesh=flat, in_specs=(rows, rows, vector, vector, vector), out_specs=(rows, vector), check_vma=False
    )
```

```python
import functools

import jax
import jax.numpy as jnp
from jax import lax
from jax.experimental import pallas as pl
from jax.experimental.pallas import tpu as pltpu
from jax.sharding import Mesh, PartitionSpec as P


loss_scale = 128.0
send_scale = 32.0
send_type = jnp.float16
width = 8192
wide = width + 256


def spans(sizes):
    return [(sum(sizes[:k]), size) for k, size in enumerate(sizes)]


middle = width // 2
f32, bf16, i32 = jnp.float32, jnp.bfloat16, jnp.int32


def device(x, y, c, z):
    return ((x * 4 + y) * 2 + c) * 8 + z


R4, R8 = range(4), range(8)
places = [(x, y, c, z) for x in R4 for y in R4 for c in (0, 1) for z in R8]
along_z = [[device(x, y, c, z) for z in R8] for x in R4 for y in R4 for c in (0, 1)]
same_core = [[device(x, y, c, z) for x in R4 for y in R4 for z in R8] for c in (0, 1)]
partner = [(device(x, y, c, z), device(x, y, 1 - c, z)) for x, y, c, z in places]


def shift(value, outer, k):
    pairs = []
    for x, y, c, z in places:
        to = device(x, (y + k) % 4, c, z) if outer == (c == 0) else device((x + k) % 4, y, c, z)
        pairs.append((device(x, y, c, z), to))
    return lax.ppermute(value, "d", pairs)


def vmem(*args):
    return pl.BlockSpec(*args) if args else pl.BlockSpec(memory_space=pltpu.VMEM)


smem = pl.BlockSpec(memory_space=pltpu.SMEM)
anywhere = pl.BlockSpec(memory_space=pl.ANY)


def pack_kernel(count_ref, mask_ref, target_ref, hidden_ref, row_ref, kept_ref, slab, sem):
    lane = lax.broadcasted_iota(i32, (1, 128), 1)
    first = jnp.min(jnp.where(mask_ref[...] == 1, lane, 127).astype(f32)).astype(i32)
    copy = pltpu.make_async_copy(hidden_ref.at[pl.ds(pl.multiple_of(first // 8 * 8, 8), 8)], slab, sem)
    copy.start()
    kept = (lane == first) & (mask_ref[...] == 1) & (count_ref[0] > 0)
    kept_ref[...] = kept.astype(i32)
    code = jnp.sum(jnp.where(kept, target_ref[...] + 1, 0).astype(f32)).astype(i32)
    wide_lane = lax.broadcasted_iota(i32, (1, 256), 1)
    digits = jnp.where(wide_lane == 0, code % 256, 0) + jnp.where(wide_lane == 1, code // 256 % 256, 0)
    digits = digits + jnp.where(wide_lane == 2, code // 65536, 0)
    copy.wait()
    take = (lax.broadcasted_iota(i32, (8, width), 0) == first % 8) & (code > 0)
    row = jnp.sum(jnp.where(take, slab[...].astype(f32), 0.0), axis=0, keepdims=True)
    half = wide // 2
    low, high = row[:, :half], jnp.concatenate([row[:, half:], digits.astype(f32)], axis=1)
    both = jnp.where(lax.broadcasted_iota(i32, (2, half), 0) == 0, low, high).astype(bf16)
    row_ref[...] = jnp.broadcast_to(both[None], row_ref.shape)


def pack(count, mask, target, hidden):
    return pl.pallas_call(
        pack_kernel,
        in_specs=[smem, vmem(), vmem(), anywhere],
        out_specs=[vmem(), vmem()],
        out_shape=[jax.ShapeDtypeStruct((8, 2, wide // 2), bf16), jax.ShapeDtypeStruct((1, 128), i32)],
        scratch_shapes=[pltpu.VMEM((8, width), bf16), pltpu.SemaphoreType.DMA],
        name="pack",
    )(count, mask.reshape(1, 128), target.reshape(1, 128), far(hidden))


def far(value):
    return pltpu.with_memory_space_constraint(value, pltpu.HBM)


def by_rank(values, i, j):
    values = pltpu.roll(values, j * 32, 1)
    lane = lax.broadcasted_iota(i32, values.shape, 1)
    return jnp.where(lane % 32 >= i * 8, pltpu.roll(values, i * 8, 1), pltpu.roll(values, (i * 8 + 96) % 128, 1))


def by_arrival(values, i, j):
    lane = lax.broadcasted_iota(i32, values.shape, 1)
    back, around = pltpu.roll(values, (128 - i * 8) % 128, 1), pltpu.roll(values, 32 - i * 8, 1)
    return pltpu.roll(jnp.where(lane % 32 < 32 - i * 8, back, around), (128 - j * 32) % 128, 1)


def fetch(pairs, sems):
    copies = [[pltpu.make_async_copy(a, b, sems.at[k, n]) for n, (a, b) in enumerate(p)] for k, p in enumerate(pairs)]
    for chunk in copies:
        for copy in chunk:
            copy.start()
    return copies


def weight_copies(chunks, start, w_ref, v_ref, weights):
    pairs = []
    for at, size in chunks:
        source, held = pl.ds(start + at, size), pl.ds(at, size)
        pairs.append([(w_ref.at[:, source], weights[0].at[:, held]), (v_ref.at[:, source], weights[1].at[:, held])])
    return pairs


def logits_kernel(half, vocab_rows, *refs):
    if half == 0:
        r0, r1, r2, r3, w_ref, v_ref, own_ref, other_ref, *weights, rows, sems = refs
        chunks = spans([1024, 1024, 2048])
    else:
        place_ref, own_in, other_in, r0, r1, r2, r3, w_ref, v_ref = refs[:9]
        own_ref, other_ref, *weights, stats_ref, target_ref, rows, sems = refs[9:]
        chunks = spans([2048, 1024, 1024])
    pairs = weight_copies(chunks, half * middle, w_ref, v_ref, weights)
    for pair, (at, size) in zip(pairs, chunks):
        extra = (wide - width) * (half == 1 and at + size == middle)
        cols = pl.ds(at, size + extra)
        pair += [(r.at[:, cols], rows.at[pl.ds(k * 32, 32), cols]) for k, r in enumerate((r0, r1, r2, r3))]
    copies = fetch(pairs, sems)
    for k, (at, size) in enumerate(chunks):
        for copy in copies[k]:
            copy.wait()
        cols = pl.ds(at, size)
        for slot, out in enumerate((own_ref, other_ref)):
            part = lax.dot_general(
                weights[slot][:, cols], rows[:, cols], (((1,), (1,)), ((), ())), preferred_element_type=f32
            )
            if k:
                part = out[...] + part
            elif half:
                part = (own_in, other_in)[slot][...] + part
            out[...] = part
    if half == 0:
        return

    i, j, me = place_ref[0], place_ref[1], place_ref[2]
    digits = rows[:, pl.ds(middle, 128)].astype(f32).T
    target = (digits[0:1] + 256 * digits[1:2] + 65536 * digits[2:3]).astype(i32) - 1
    top = jnp.maximum(jnp.max(own_ref[...], axis=0, keepdims=True), jnp.max(other_ref[...], axis=0, keepdims=True))
    total, pick = 0.0, 0.0
    for out, base in ((own_ref, me), (other_ref, me ^ 8)):
        ids = lax.broadcasted_iota(i32, (vocab_rows, 128), 0) + base * vocab_rows
        total += jnp.sum(jnp.exp(out[...] - top), axis=0, keepdims=True)
        pick += jnp.sum(jnp.where(ids == target, out[...], 0.0), axis=0, keepdims=True)
    row = lax.broadcasted_iota(i32, (8, 128), 0)
    stats = jnp.where(row == 0, top + jnp.log(total), pick)
    stats_ref[...] = jnp.broadcast_to(by_rank(stats, i, j)[None, :2], stats_ref.shape)
    target_ref[...] = target


def logits_call(half, place, partial, rows, own, other):
    vocab_rows = own.shape[0]
    partial_shape = [jax.ShapeDtypeStruct((vocab_rows, 128), f32)] * 2 + [pltpu.VMEM((vocab_rows, middle), bf16)] * 2
    stats_shape = [jax.ShapeDtypeStruct((128, 2, 128), f32), jax.ShapeDtypeStruct((1, 128), i32)]
    return pl.pallas_call(
        functools.partial(logits_kernel, half, vocab_rows),
        in_specs=([smem] + [vmem()] * 2) * half + [anywhere] * 6,
        out_specs=[vmem()] * (6 if half else 4),
        out_shape=partial_shape + stats_shape * half,
        scratch_shapes=[
            pltpu.VMEM((128, middle + (wide - width) * half), bf16),
            pltpu.SemaphoreType.DMA((3, 6)),
        ],
        compiler_params=pltpu.CompilerParams(vmem_limit_bytes=8 << 20),
    )(*(([place] + list(partial)) if half else []), *rows, far(own), far(other))


def coefficient_kernel(vocab_rows, place_ref, target_ref, stats_ref, own_ref, other_ref, loss_ref, own_coef, other_coef):
    i, j, me = place_ref[0], place_ref[1], place_ref[2]
    lse = stats_ref[:, 0, :]
    top = jnp.max(lse, axis=0, keepdims=True)
    log_total = top + jnp.log(jnp.sum(jnp.exp(lse - top), axis=0, keepdims=True))
    picked = jnp.sum(stats_ref[:, 1, :], axis=0, keepdims=True)
    target = target_ref[...]
    loss_ref[...] = log_total - picked
    log_total = by_arrival(jnp.broadcast_to(log_total, (8, 128)), i, j)[0:1]
    for logits, coef, base in ((own_ref, own_coef, me), (other_ref, other_coef, me ^ 8)):
        ids = lax.broadcasted_iota(i32, (vocab_rows, 128), 0) + base * vocab_rows
        hit = (ids == target).astype(f32)
        coef[...] = jnp.where(target >= 0, jnp.exp(logits[...] - log_total) - hit, 0.0).T.astype(bf16)


def coefficient_call(place, target, stats, logits):
    vocab_rows = logits[0].shape[0]
    return pl.pallas_call(
        functools.partial(coefficient_kernel, vocab_rows),
        in_specs=[smem] + [vmem()] * 4,
        out_specs=[vmem()] * 3,
        out_shape=[jax.ShapeDtypeStruct((1, 128), f32)] + [jax.ShapeDtypeStruct((128, vocab_rows), bf16)] * 2,
        compiler_params=pltpu.CompilerParams(vmem_limit_bytes=4 << 20),
        name="coefficient",
    )(place, target, stats, *logits)


def exchange(value, groups):
    return lax.all_to_all(value, "d", 0, 0, axis_index_groups=groups)


def gather4(value, outer):
    far, back, on = shift(value, outer, 2), shift(value, outer, 1), shift(value, outer, 3)
    return [value, on, far, back]


def reduce4(blocks, outer):
    far, on, back = shift(blocks[2], outer, 2), shift(blocks[1], outer, 1), shift(blocks[3], outer, 3)
    return (blocks[0].astype(f32) + on.astype(f32)) + (far.astype(f32) + back.astype(f32))


def shards(hidden, out_weight, loss_mask, targets, kept_count):
    me = lax.axis_index("d")
    z, c, y, x = me % 8, (me // 8) % 2, (me // 16) % 4, me // 64
    i, j = jnp.where(c == 0, x, y), jnp.where(c == 0, y, x)
    place = jnp.stack([i, j, me])
    other_weight = lax.ppermute(out_weight, "d", partner)

    packed, kept = pack(kept_count, loss_mask, targets, hidden)
    rows = gather4(exchange(packed, along_z).reshape(8, wide), False)
    halves = [jnp.concatenate([r[:, a:b] for r in rows], axis=0) for a, b in ((0, middle), (middle, wide))]
    first = gather4(halves[0], True)
    halves = [first, gather4(halves[1], True)]
    *partial, own, other = logits_call(0, place, None, halves[0], out_weight, other_weight)
    near = [(own, other)]
    *logits, own, other, stats, target = logits_call(1, place, partial, halves[1], out_weight, other_weight)
    near.append((own, other))
    stats = exchange(stats, same_core)
    loss, *coefs = coefficient_call(place, target, stats, logits)
    parts = []
    for weights in near:
        grad = sum(jnp.dot(k, w, preferred_element_type=f32) for k, w in zip(coefs, weights))
        grad = (grad * (loss_scale * send_scale)).astype(send_type)
        parts.append(reduce4([grad[k * 32:(k + 1) * 32] for k in R4], True))
    part = jnp.concatenate(parts, axis=1).astype(send_type)
    part = reduce4([part[k * 8:(k + 1) * 8] for k in R4], False)
    part = exchange(part.astype(send_type).reshape(8, width // 128, 128), along_z)
    own_grad = (jnp.sum(part.astype(f32), axis=0) * (1.0 / send_scale)).reshape(1, width)

    own_loss = lax.dynamic_slice_in_dim(loss[0], (j * 4 + i) * 8 + z, 1, 0)
    kept_row = kept[0] > 0
    hidden_grad = jnp.where(kept_row[:, None], own_grad, 0.0).astype(bf16)
    row_loss = jnp.where(kept_row, own_loss, 0.0)
    return hidden_grad, row_loss


def solution(mesh):
    flat = Mesh(mesh.devices.reshape(-1), ("d",))
    rows = P("d", None)
    vector = P("d")
    return jax.shard_map(
        shards, mesh=flat, in_specs=(rows, rows, vector, vector, vector), out_specs=(rows, vector), check_vma=False
    )
```
